32 devices in a mesh: region: 4 (over x, core), pair: 8 (over z, y).
Axes of the slice: x: 2, y: 2, z: 4, core: 2. Of those that a mesh axis runs over, the one named last changes fastest.
Arguments:
- points: float32 [3, 8192, 128], P(None, ('region', 'pair')), may hold values from -6 to 6
- offsets: float32 [3, 8192, 128], P(None, ('region', 'pair')), may hold values from -12 to 12
- normals: float32 [3, 8192, 128], P(None, ('region', 'pair')), may hold values from -6 to 6
- block_count: int32 [8192], P(('region', 'pair')), may hold values from 0 to 128, as said below
- block_edge: int32 [8192], P(('region', 'pair')), may hold values from 0 to 63
- edge_scan: int32 [2048], P(('region', 'pair')), may hold values from 0 to 127
- edge_nbr: int32 [2048], P(('region', 'pair')), may hold values from 0 to 383, as said below
- rotvec: float32 [3, 4096], P(None, ('region', 'pair')), may hold values from -0.3 to 0.3
Outputs:
- edge_pose: float32 [6, 2048], P(None, ('region', 'pair'))
- rotations: float32 [9, 4096], P(None, ('region', 'pair'))
The draws below stay inside these ranges and needn't reach their ends.
Inputs may be any that keep to these rules, and one draw needn't show every extreme that they name: `block_count`: some block is full in every draw; a count of 0 marks an empty slot. `edge_nbr`: values below 128 name a scan of the device one step lower along region, values from 256 one of the device one step higher, the rest one of the device's own scans other than the slot's own scan; devices at the ends of region name no missing neighbour.
All inputs are finite; a program needn't handle non-finite values.
Results may differ from the reference program's by a relative error of at most 0.0003.
Values sent between devices are 32-bit elements; how exact they have to be, the bound alone decides.
A program may use at most 64 MiB of HBM per device.

```python
import jax
import jax.numpy as jnp
from jax import lax

PTS = 128
PSLOT = 2
SLOT = 8
SCAN_DEV = 128
SWEEPS = 2
EDGE_DEV = 64
BLOCKS = 8192
EDGES = 2048
SCANS = 4096
N_REGION = 4
N_PAIR = 8


def edge_helper(key):
    first, second, third = jax.random.split(jax.random.fold_in(key, 7), 3)
    own_scan = jax.random.randint(first, (EDGES,), 0, SCAN_DEV)
    device_of = jnp.arange(EDGES, dtype=jnp.int32) // EDGE_DEV
    region_of = device_of // N_PAIR
    low_side = jnp.where(region_of == 0, 1, 0)
    high_side = jnp.where(region_of == N_REGION - 1, 2, 3)
    side = low_side + jax.random.randint(second, (EDGES,), 0, 1 << 20) % (high_side - low_side)
    offset = jax.random.randint(third, (EDGES,), 0, SCAN_DEV)
    offset = jnp.where((side == 1) & (offset == own_scan), (offset + 1) % SCAN_DEV, offset)
    neighbor = side * SCAN_DEV + offset
    neighbor = neighbor.at[0].set(3 * SCAN_DEV - 1)
    neighbor = neighbor.at[(N_REGION * N_PAIR - 1) * EDGE_DEV].set(0)
    own_scan = own_scan.at[0].set(0)
    return (own_scan.astype(jnp.int32), neighbor.astype(jnp.int32))


def draw_edge_scan(key, part):
    return edge_helper(key)[0]


def draw_edge_nbr(key, part):
    return edge_helper(key)[1]


def draw_block_count(key, part):
    counts = jax.random.randint(jax.random.fold_in(key, 3), (BLOCKS,), 0, PTS + 1)
    return counts.at[0].set(PTS).astype(jnp.int32)


def place_ends(values, rng, least, high):
    shape = values.shape
    spot = [jax.random.randint(jax.random.fold_in(rng, axis), (), 0, shape[axis]) for axis in range(len(shape))]
    values = values.at[tuple(spot)].set(least)
    longest = shape.index(max(shape))
    spot[longest] = (spot[longest] + 1) % shape[longest]
    return values.at[tuple(spot)].set(high)


def block_scale(key, extent, cuts, smallest, largest):
    gain, own = 1.0, jax.random.fold_in(key, 6)
    for dim, parts in cuts:
        heights = jnp.exp(jax.random.uniform(jax.random.fold_in(own, dim), (parts,), jnp.float32, smallest / len(cuts), largest / len(cuts)))
        gain = gain * jnp.repeat(heights, extent[dim] // parts).reshape([-1 if axis == dim else 1 for axis in range(len(extent))])
    return gain


def bell_draw(stream_key, shape, deviation, limit, shards=(), held_as=jnp.bfloat16):
    factor_of = block_scale(stream_key, shape, shards, -0.22, 0.18) if shards else 1.0
    values = jax.random.normal(stream_key, shape, jnp.float32) * deviation * factor_of
    return jnp.minimum(jnp.maximum(values, -limit), limit).astype(held_as)


def setup_inputs(seed: int = 0) -> dict:
    key_list = jax.random.split(jax.random.key(seed), 9)
    points = bell_draw(key_list[0], (3, BLOCKS, PTS), 1.0, 6.0, ((1, 32),), jnp.float32)
    offsets = bell_draw(key_list[1], (3, BLOCKS, PTS), 2.0, 12.0, ((1, 32),), jnp.float32)
    normals = bell_draw(key_list[2], (3, BLOCKS, PTS), 1.0, 6.0, ((1, 32),), jnp.float32)
    block_count = draw_block_count(jax.random.fold_in(key_list[8], 71), 0)
    block_edge = place_ends(jax.random.randint(key_list[4], (BLOCKS,), 0, EDGE_DEV), jax.random.fold_in(key_list[4], 1), 0, EDGE_DEV - 1).astype(jnp.int32)
    edge_scan = draw_edge_scan(jax.random.fold_in(key_list[8], 71), 0)
    edge_nbr = draw_edge_nbr(jax.random.fold_in(key_list[8], 71), 0)
    rotvec = jnp.clip(jax.random.uniform(key_list[7], (3, SCANS), jnp.float32, -0.3, 0.3) * block_scale(key_list[7], (3, SCANS), ((1, 32),), -0.4, 0.0), -0.3, 0.3)
    return {"points": points, "offsets": offsets, "normals": normals, "block_count": block_count, "block_edge": block_edge, "edge_scan": edge_scan, "edge_nbr": edge_nbr, "rotvec": rotvec}


damping = 16.0
min_length = 0.1

def exp_rotation(vector):
    theta_sq = vector[0] * vector[0] + vector[1] * vector[1] + vector[2] * vector[2]
    first = 1.0 - theta_sq / 6.0 + theta_sq ** 2 / 120.0 - theta_sq ** 3 / 5040.0 + theta_sq ** 4 / 362880.0
    second = 0.5 - theta_sq / 24.0 + theta_sq ** 2 / 720.0 - theta_sq ** 3 / 40320.0 + theta_sq ** 4 / 3628800.0
    skew_rows = [[None, -vector[2], vector[1]], [vector[2], None, -vector[0]], [-vector[1], vector[0], None]]
    entries = []
    for row in range(3):
        for col in range(3):
            value = second * vector[row] * vector[col]
            if row == col:
                value = value + 1.0 - second * theta_sq
            else:
                value = value + first * skew_rows[row][col]
            entries.append(value)
    return jnp.stack(entries)

def log_rotation(matrix):
    cosine = (matrix[0] + matrix[4] + matrix[8] - 1.0) * 0.5
    axis_vec = 0.5 * jnp.stack([matrix[7] - matrix[5], matrix[2] - matrix[6], matrix[3] - matrix[1]])
    sine = jnp.sqrt(lax.optimization_barrier(jnp.sum(axis_vec * axis_vec, axis=0)))
    theta = jnp.arctan2(sine, cosine)
    factor = jnp.where(sine < 0.0001, 1.0 + sine * sine / 6.0, theta / jnp.maximum(sine, 0.0001))
    return factor * axis_vec

def mat_mul(left, right):
    return jnp.stack([sum((left[3 * a + b] * right[3 * b + c] for b in range(3))) for a in range(3) for c in range(3)])

def mat_tmul(left, right):
    return jnp.stack([sum((left[3 * b + a] * right[3 * b + c] for b in range(3))) for a in range(3) for c in range(3)])

def solve_six(matrix, rhs):
    lower = [[None] * 6 for _ in range(6)]
    for col in range(6):
        diag_val = matrix[col, col] - sum((lower[col][k] * lower[col][k] for k in range(col))) if col else matrix[col, col]
        lower[col][col] = jnp.sqrt(diag_val)
        for row in range(col + 1, 6):
            value = matrix[row, col] - sum((lower[row][k] * lower[col][k] for k in range(col))) if col else matrix[row, col]
            lower[row][col] = value / lower[col][col]
    inter = []
    for row in range(6):
        value = rhs[row] - sum((lower[row][k] * inter[k] for k in range(row))) if row else rhs[row]
        inter.append(value / lower[row][row])
    result = [None] * 6
    for row in range(5, -1, -1):
        value = inter[row] - sum((lower[k][row] * result[k] for k in range(row + 1, 6))) if row < 5 else inter[row]
        result[row] = value / lower[row][row]
    return jnp.stack(result)

def normal_terms(src_pts, offset, normal):
    cross = jnp.stack([src_pts[1] * normal[2] - src_pts[2] * normal[1], src_pts[2] * normal[0] - src_pts[0] * normal[2], src_pts[0] * normal[1] - src_pts[1] * normal[0]])
    jacobian = jnp.concatenate([cross, normal], axis=0)
    resid = lax.optimization_barrier(jnp.sum(normal * offset, axis=0))
    hess = jnp.einsum('ibw,jbw->ijb', jacobian, jacobian, precision=lax.Precision.HIGHEST)
    grad = jnp.einsum('ibw,bw->ib', jacobian, resid, precision=lax.Precision.HIGHEST)
    return jnp.concatenate([hess.reshape(36, -1), grad], axis=0)

def slot_table(block_edge, count):
    return (block_edge[:, None] == jnp.arange(count, dtype=jnp.int32)[None, :]).astype(jnp.float32)

def slot_sums(terms, block_edge, count):
    return jnp.dot(terms, slot_table(block_edge, count), precision=lax.Precision.HIGHEST)

def slot_live(filled, block_edge, count):
    hits = jnp.dot(filled[None, :], slot_table(block_edge, count), precision=lax.Precision.HIGHEST)[0]
    return (hits > 0.5).astype(jnp.float32)

def solve_poses(sums):
    hess = sums[:36].reshape(6, 6, -1) + damping * jnp.eye(6, dtype=jnp.float32)[:, :, None]
    return -solve_six(hess, sums[36:])

def reference(points, offsets, normals, block_count, block_edge, edge_scan, edge_nbr, rotvec):
    devices = N_REGION * N_PAIR

    def by_owner(array):
        return array.reshape(3, devices, devices, SLOT, PTS).transpose(2, 0, 1, 3, 4).reshape(devices, 3, devices * SLOT, PTS)

    def ints_by_owner(array):
        return array.reshape(devices, devices, SLOT).transpose(1, 0, 2).reshape(devices, devices * SLOT)

    def one_owner(items):
        src_pts, offset, normal, count, owner_edge = items
        width = jnp.arange(PTS, dtype=jnp.int32)
        block_mask = (width[None, :] < count[:, None]).astype(jnp.float32)[None]
        terms = normal_terms(src_pts * block_mask, offset * block_mask, normal * block_mask)
        filled = (count > 0).astype(jnp.float32)
        return (slot_sums(terms, owner_edge, EDGE_DEV), slot_live(filled, owner_edge, EDGE_DEV))
    sums, live_mask = lax.map(one_owner, (by_owner(points), by_owner(offsets), by_owner(normals), ints_by_owner(block_count), ints_by_owner(block_edge)))
    sums = sums.reshape(devices, 42, devices, PSLOT).transpose(1, 2, 0, 3).reshape(42, EDGES)
    live_mask = live_mask.reshape(devices, devices, PSLOT).transpose(1, 0, 2).reshape(EDGES)
    pose_out = solve_poses(sums)
    relative = exp_rotation(pose_out[:3])
    device_of = jnp.arange(EDGES, dtype=jnp.int32) // EDGE_DEV
    scan_glob = device_of * SCAN_DEV + edge_scan
    nbr_glob = (device_of + (edge_nbr // SCAN_DEV - 1) * N_PAIR) * SCAN_DEV + edge_nbr % SCAN_DEV
    rotation = exp_rotation(rotvec)
    for sweep in range(SWEEPS):
        near = jnp.take(rotation, nbr_glob, axis=1)
        mine = jnp.take(rotation, scan_glob, axis=1)
        tangent = log_rotation(mat_tmul(mine, mat_mul(near, relative)))
        length = jnp.sqrt(lax.optimization_barrier(jnp.sum(tangent * tangent, axis=0)))
        weight = live_mask / jnp.maximum(length, min_length)
        numer = jax.ops.segment_sum((weight * tangent).T, scan_glob, SCANS).T
        denom = jax.ops.segment_sum(weight, scan_glob, SCANS) + 1.0
        rotation = mat_mul(rotation, exp_rotation(numer / denom))
    return (pose_out, rotation)
```

```python
import functools
import math

import jax
import jax.numpy as jnp
from jax import lax
from jax.experimental import pallas as pl
from jax.experimental.pallas import tpu as pltpu
from jax.sharding import PartitionSpec as P

damping = 16.0
min_length = 0.1
MESH = pl.DeviceIdType.MESH
F32 = jnp.float32
BF16 = jnp.bfloat16
ROWS = 32
KEPT = 4


def owners(regions, pairs):
    near = sorted(
        ((r, p) for r in range(regions) for p in range(pairs)),
        key=lambda at: (at[0] // 2 + at[1] // 2 + at[1] % 2, at[0] // 2, at[1], at[0]),
    )
    return sorted(near[: regions * pairs // KEPT])


def exp_rotation(v):
    t = v[0] * v[0] + v[1] * v[1] + v[2] * v[2]
    a = 1.0 + t * (-1.0 / 6.0 + t * (1.0 / 120.0 + t * (-1.0 / 5040.0 + t * (1.0 / 362880.0))))
    b = 0.5 + t * (-1.0 / 24.0 + t * (1.0 / 720.0 + t * (-1.0 / 40320.0 + t * (1.0 / 3628800.0))))
    bv = [b * v[i] for i in range(3)]
    av = [a * v[i] for i in range(3)]
    diag = 1.0 - b * t
    xy, xz, yz = bv[0] * v[1], bv[0] * v[2], bv[1] * v[2]
    return [
        diag + bv[0] * v[0], xy - av[2], xz + av[1],
        xy + av[2], diag + bv[1] * v[1], yz - av[0],
        xz - av[1], yz + av[0], diag + bv[2] * v[2],
    ]


def angle(s, c):
    size = jnp.abs(c)
    big, small = jnp.maximum(s, size), jnp.minimum(s, size)
    far = small > 0.41421356 * big
    z = jnp.where(far, small - big, small) / jnp.maximum(jnp.where(far, small + big, big), 1e-30)
    z2 = z * z
    poly = ((8.05374449538e-2 * z2 - 1.38776856032e-1) * z2 + 1.99777106478e-1) * z2 - 3.33329491539e-1
    r = jnp.where(far, math.pi / 4, 0.0) + (z + z * z2 * poly)
    r = jnp.where(s > size, math.pi / 2 - r, r)
    return jnp.where(c < 0.0, math.pi - r, r)


def log_rotation(m):
    c = (m[0] + m[4] + m[8] - 1.0) * 0.5
    u = [0.5 * (m[7] - m[5]), 0.5 * (m[2] - m[6]), 0.5 * (m[3] - m[1])]
    s2 = u[0] * u[0] + u[1] * u[1] + u[2] * u[2]
    s = jnp.sqrt(s2)
    f = jnp.where(s < 0.0001, 1.0 + s2 / 6.0, angle(s, c) / jnp.maximum(s, 0.0001))
    return [f * x for x in u]


def mat_mul(x, y):
    return [sum(x[3 * a + b] * y[3 * b + c] for b in range(3)) for a in range(3) for c in range(3)]


def mat_tmul(x, y):
    return [sum(x[3 * b + a] * y[3 * b + c] for b in range(3)) for a in range(3) for c in range(3)]


def split_pair(x):
    hi = x.astype(BF16)
    mid = (x - hi.astype(F32)).astype(BF16)
    return jnp.concatenate([hi, mid], axis=0)


def exact_dot(x, table, dims):
    rows = x.shape[0]
    out = lax.dot_general(split_pair(x), table, (dims, ((), ())), preferred_element_type=F32)
    return out[:rows] + out[rows:]


def one_hot(index, count, width):
    grid = lax.broadcasted_iota(jnp.int32, (count, width), 0)
    return jnp.where(grid == index, 1.0, 0.0).astype(BF16)


def solve(h, g):
    low = [[None] * 6 for _ in range(6)]
    val = [[None] * 6 for _ in range(6)]
    inv = [None] * 6
    for c in range(6):
        for r in range(c, 6):
            x = h[r][c]
            for k in range(c):
                x = x - val[r][k] * low[c][k]
            val[r][c] = x
        inv[c] = 1.0 / val[c][c]
        for r in range(c + 1, 6):
            low[r][c] = val[r][c] * inv[c]
    y = []
    for r in range(6):
        x = g[r]
        for k in range(r):
            x = x - low[r][k] * y[k]
        y.append(x)
    out = [None] * 6
    for r in range(5, -1, -1):
        x = y[r] * inv[r]
        for k in range(r + 1, 6):
            x = x - low[k][r] * out[k]
        out[r] = x
    return out


def kernel(
    sizes,
    pts_hbm, off_hbm, nrm_hbm, cnt_hbm, edge_hbm, scan_ref, nbr_ref, rv_ref,
    pose_ref, rot_ref,
    data, tr, tt, tab, send1, recv1, sums_ref, poses, groups, send2, recv2, rows2,
    rvh, sch, nbh, near_tab, own_tab, cnt_ref, edge_ref,
    in_sem, int_sem, s1, r1, s2, r2, hs, hr, es, er, ns, nr,
):
    regions, pairs, blocks, edges, scans = sizes
    n = regions * pairs
    slot = blocks // n
    per = edges // n
    per_row = 128 // ROWS
    m1 = slot * ROWS // 128
    ep = max(edges, 128)
    halves = blocks // 128
    reg, pair = lax.axis_index("region"), lax.axis_index("pair")
    me = reg * pairs + pair

    def wrapped(x, size):
        return jnp.where(x >= size, x - size, x)

    mids = owners(regions, pairs)

    def holds(r, p):
        hit = [jnp.logical_and(r == a, p == b) for a, b in mids]
        return functools.reduce(jnp.logical_or, hit)

    is_mid = holds(reg, pair)
    rank = sum(jnp.where(me == r * pairs + p, k, 0) for k, (r, p) in enumerate(mids))
    beside = sorted({k % regions for k in (-2, -1, 1, 2)})

    def each_mid(send):
        @pl.when(is_mid)
        def _():
            for k, where in enumerate(mids):
                @pl.when(rank != k)
                def _():
                    send(k, where)

        @pl.when(jnp.logical_not(is_mid))
        def _():
            for k, where in enumerate(mids):
                send(k, where)

    def each_other(send):
        def step(dp, carry):
            p = wrapped(pair + pairs - dp, pairs)
            for dr in range(regions):
                r = wrapped(reg + dr, regions)
                send(r * pairs + p, (r, p))
            return carry

        for dr in range(1, regions):
            r = wrapped(reg + dr, regions)
            send(r * pairs + pair, (r, pair))
        lax.fori_loop(1, pairs, step, 0)

    ints = [
        pltpu.make_async_copy(cnt_hbm, cnt_ref, int_sem.at[0]),
        pltpu.make_async_copy(edge_hbm, edge_ref, int_sem.at[1]),
    ]
    for copy in ints:
        copy.start()
    loads = []
    for h in range(halves):
        for a, ref in enumerate((pts_hbm, off_hbm, nrm_hbm)):
            copy = pltpu.make_async_copy(
                ref.at[:, pl.ds(h * 128, 128), :], data.at[h, a], in_sem.at[h, a]
            )
            copy.start()
            loads.append(copy)

    barrier = pltpu.get_barrier_semaphore()


    def greet(to, where):
        pl.semaphore_signal(barrier, inc=1, device_id=where, device_id_type=MESH)

    sides = [wrapped(reg + dr, regions) for dr in beside]
    apart = [jnp.logical_not(holds(r, pair)) for r in sides]

    @pl.when(is_mid)
    def _():
        each_other(greet)

    @pl.when(jnp.logical_not(is_mid))
    def _():
        for r, p in mids:
            greet(r * pairs + p, (r, p))
        for r, other in zip(sides, apart):
            @pl.when(other)
            def _():
                greet(r, (r, pair))

    groups[...] = jnp.zeros_like(groups)
    poses[...] = jnp.zeros_like(poses)
    sums_ref[...] = jnp.zeros_like(sums_ref)
    tt[...] = jnp.zeros_like(tt)
    rvh[pl.ds(5, 3)] = jnp.zeros((3, 3, scans), F32)
    rows2[...] = jnp.zeros_like(rows2)
    for copy in ints:
        copy.wait()
    for h in range(halves):
        for a in range(3):
            loads[3 * h + a].wait()
            for c in range(3):
                tr[3 * a + c] = data[h, a, c].T
        count = cnt_ref[:, h * 128 : (h + 1) * 128]

        def chunk(i, acc):
            acc = list(acc)
            for u in range(2):
                at = pl.multiple_of(i * 16 + u * 8, 8)
                p = [tr[c, pl.ds(at, 8), :] for c in range(3)]
                d = [tr[3 + c, pl.ds(at, 8), :] for c in range(3)]
                live = lax.broadcasted_iota(jnp.int32, (8, 128), 0) + at < count
                v = [jnp.where(live, tr[6 + c, pl.ds(at, 8), :], 0.0) for c in range(3)]
                jac = [
                    p[1] * v[2] - p[2] * v[1],
                    p[2] * v[0] - p[0] * v[2],
                    p[0] * v[1] - p[1] * v[0],
                ] + v
                resid = v[0] * d[0] + v[1] * d[1] + v[2] * d[2]
                at_t = 0
                for x in range(6):
                    for y in range(x + 1):
                        acc[at_t] = acc[at_t] + jac[x] * jac[y]
                        at_t += 1
                for x in range(6):
                    acc[21 + x] = acc[21 + x] + jac[x] * resid
            return tuple(acc)

        acc = lax.fori_loop(0, 8, chunk, tuple(jnp.zeros((8, 128), F32) for _ in range(27)))
        for t in range(27):
            tt[t : t + 1, :] = jnp.sum(acc[t], axis=0, keepdims=True)
        tt[27:28, :] = jnp.where(count > 0, 1.0, 0.0)
        tt[28:29, :] = edge_ref[:, h * 128 : (h + 1) * 128].astype(F32)
        tab[pl.ds(h * 128, 128), :] = tt[...].T
    for j in range(m1):
        row = tab[pl.ds(j * per_row, n, stride=slot), :]
        for k in range(1, per_row):
            row = row + pltpu.roll(tab[pl.ds(j * per_row + k, n, stride=slot), :], ROWS * k, 1)
        send1[:, j, :] = row

    @pl.when(is_mid)
    def _():
        pl.semaphore_wait(barrier, n - 1)

    @pl.when(jnp.logical_not(is_mid))
    def _():
        pl.semaphore_wait(barrier, len(mids) + sum(other.astype(jnp.int32) for other in apart))

    each_mid(
        lambda k, where: pltpu.make_async_remote_copy(
            send1.at[pl.ds(k * KEPT, KEPT)], recv1.at[me], s1, r1, device_id=where, device_id_type=MESH
        ).start()
    )

    @pl.when(is_mid)
    def _():
        pltpu.make_async_copy(send1.at[pl.ds(rank * KEPT, KEPT)], recv1.at[me], r1).start()

    for k in (-1, 1, -2, 2):
        where = (wrapped(reg + k % regions, regions), pair)
        pltpu.make_async_remote_copy(
            rv_ref, rvh.at[2 - k], hs, hr, device_id=where, device_id_type=MESH
        ).start()
        if abs(k) == 1:
            pltpu.make_async_remote_copy(
                scan_ref, sch.at[1 - k], es, er, device_id=where, device_id_type=MESH
            ).start()
            pltpu.make_async_remote_copy(
                nbr_ref, nbh.at[1 - k], ns, nr, device_id=where, device_id_type=MESH
            ).start()
    pltpu.make_async_copy(rv_ref, rvh.at[2], hr).start()
    pltpu.make_async_copy(scan_ref, sch.at[1], er).start()
    pltpu.make_async_copy(nbr_ref, nbh.at[1], nr).start()

    @pl.when(is_mid)
    def _():
        pltpu.make_async_copy(recv1, recv1, r1).wait()
        wide = max(edges, 128)
        span = wide // edges
        lanes = m1 * n
        for q in range(KEPT // span):
            got = [recv1[:, q * span + h, j, :] for h in range(span) for j in range(m1)]
            got = jnp.concatenate(got, axis=0)
            turned_rows = [got[128 * i : 128 * (i + 1)].T for i in range(span * lanes // 128)]
            turned_rows = jnp.concatenate(turned_rows, axis=1) if len(turned_rows) > 1 else turned_rows[0]
            mine = [turned_rows[ROWS * k : ROWS * (k + 1)] for k in range(per_row)]
            owner = lax.broadcasted_iota(jnp.int32, (1, span * lanes), 1) // lanes * edges
            offset = owner.astype(F32)
            slots = lax.broadcasted_iota(jnp.int32, (wide, span * lanes), 0).astype(F32)
            table = [jnp.where(slots == x[28:29] + offset, 1.0, 0.0).astype(BF16) for x in mine]
            total = exact_dot(
                jnp.concatenate(mine, axis=1), jnp.concatenate(table, axis=1), ((1,), (1,))
            )
            for i in range(wide // 128):
                sums_ref[pl.ds(q * (wide // 128) + i, ROWS, stride=8), :] = total[:, 128 * i : 128 * (i + 1)]
        sets = KEPT * edges // 128
        h, at_t = [[None] * 6 for _ in range(6)], 0
        for x in range(6):
            for y in range(x + 1):
                h[x][y] = sums_ref[8 * at_t : 8 * at_t + 8, :] + (damping if x == y else 0.0)
                at_t += 1
        pose = [-x for x in solve(h, [sums_ref[8 * (21 + x) : 8 * (22 + x), :] for x in range(6)])]
        payload = pose + [jnp.where(sums_ref[8 * 27 : 8 * 28, :] > 0.5, 1.0, 0.0)]
        for t in range(7):
            poses[1, sets * t : sets * (t + 1), :] = payload[t][:sets]
        stacked = poses[1]

        def turned(x, by):
            if edges <= 128:
                lane = lax.rem(lax.broadcasted_iota(jnp.int32, x.shape, 1), edges)
                one = pltpu.roll(x, by, 1)
                two = pltpu.roll(x, (by - edges) % 128, 1)
                return jnp.where(lane < by, two, one)
            part = edges // 128
            row = lax.rem(lax.broadcasted_iota(jnp.int32, x.shape, 0), part)
            tall = x.shape[0]

            def moved(k):
                back = k % part
                if back == 0:
                    return x
                return jnp.where(
                    row >= back, pltpu.roll(x, back, 0), pltpu.roll(x, (back - part) % tall, 0)
                )

            lane = lax.broadcasted_iota(jnp.int32, x.shape, 1)
            whole, rest = by // 128, by % 128
            if rest == 0:
                return moved(whole)
            return jnp.where(
                lane < rest, pltpu.roll(moved(whole + 1), rest, 1), pltpu.roll(moved(whole), rest, 1)
            )

        poses[0] = turned(stacked, per * pairs)
        poses[2] = turned(stacked, edges - per * pairs)
        for q in range(sets):
            for g in range(3):
                groups[q, pl.ds(g, 8, stride=4), :] = poses[g, pl.ds(q, 8, stride=sets), :]
        held = 128 // ROWS
        for q in range(0, sets, held):
            some = range(q, min(q + held, sets))
            flat = jnp.concatenate([groups[i] for i in some], axis=0)
            if len(some) < held:
                flat = jnp.concatenate([flat, jnp.zeros((128 - ROWS * len(some), 128), F32)], axis=0)
            tab[pl.ds(128 * (q // held), 128), :] = flat.T
        for j in range(per):
            if edges <= 128:
                row = tab[pl.ds(j, n, stride=per), :]
                for h2 in range(1, span):
                    row = row + pltpu.roll(tab[pl.ds(h2 * edges + j, n, stride=per), :], ROWS * sets * h2, 1)
                send2[:, j, 0, :] = row
            else:
                part = edges // 128
                count = 128 // per
                for i in range(sets // held):
                    block = tab[pl.ds(128 * i + j, count, stride=per), :]
                    for b in range(part):
                        send2[pl.ds(b * count, count), j, i, :] = pltpu.roll(block, (128 - ROWS * b) % 128, 1)
        each_other(
            lambda to, where: pltpu.make_async_remote_copy(
                send2.at[to], recv2.at[rank], s2, r2, device_id=where, device_id_type=MESH
            ).start()
        )
        pltpu.make_async_copy(send2.at[me], recv2.at[rank], r2).start()

    pltpu.make_async_copy(rvh.at[pl.ds(0, 5)], rvh.at[pl.ds(0, 5)], hr).wait()
    pltpu.make_async_copy(sch, sch, er).wait()
    pltpu.make_async_copy(nbh, nbh, nr).wait()
    for q in range(3):
        near_tab[:, q * ep : q * ep + edges] = one_hot(nbh[q], 3 * scans, edges)
        own_tab[:, q * ep : q * ep + edges] = one_hot(sch[q], scans, edges)
        if ep > edges:
            near_tab[:, q * ep + edges : (q + 1) * ep] = jnp.zeros((3 * scans, ep - edges), BF16)
            own_tab[:, q * ep + edges : (q + 1) * ep] = jnp.zeros((scans, ep - edges), BF16)

    def up(x, k):
        return pltpu.roll(x, (8 - k) % 8, 0) if k % 8 else x

    def picked(out, c, sets, width):
        block = out[8 * c : 8 * c + 8]
        if len(sets) == 1:
            return block
        value = block[:, :width]
        for q in sets[1:]:
            value = jnp.where(
                lax.broadcasted_iota(jnp.int32, (8, width), 0) == q,
                block[:, q * width : (q + 1) * width],
                value,
            )
        return value

    def between(rot, sets, shift):
        cols = pl.ds(sets[0] * ep, len(sets) * ep)
        parts = [
            jnp.concatenate([up(x, s + shift) for x in rot], axis=0) for s in range(3)
        ]
        near = exact_dot(jnp.concatenate(parts, axis=1), near_tab[:, cols], ((1,), (0,)))
        mine = exact_dot(parts[1], own_tab[:, cols], ((1,), (0,)))
        return mat_tmul(
            [picked(mine, c, sets, ep) for c in range(9)],
            [picked(near, c, sets, ep) for c in range(9)],
        )

    def step(rot, link, relative, live, sets):
        cols = pl.ds(sets[0] * ep, len(sets) * ep)
        tangent = log_rotation(mat_mul(link, relative))
        length = jnp.sqrt(tangent[0] * tangent[0] + tangent[1] * tangent[1] + tangent[2] * tangent[2])
        weight = live / jnp.maximum(length, min_length)
        weighed = jnp.concatenate([weight * x for x in tangent] + [weight], axis=0)
        parts = [
            exact_dot(weighed, own_tab[:, pl.ds(q * ep, ep)], ((1,), (1,))) for q in sets
        ]
        total = jnp.concatenate(parts, axis=1)
        numer = [picked(total, c, sets, scans) for c in range(3)]
        scale = 1.0 / (picked(total, 3, sets, scans) + 1.0)
        return mat_mul(rot, exp_rotation([x * scale for x in numer]))

    first = exp_rotation([rvh[:, c, :] for c in range(3)])
    everyone = (0, 1, 2)
    link = between(first, everyone, 0)
    base = [up(x, 1) for x in first]

    pltpu.make_async_copy(recv2, recv2, r2).wait()
    part = max(edges // 128, 1)
    span = max(128 // edges, 1)
    sets = KEPT * edges // 128
    for o in range(KEPT):
        lane, row = (ROWS * (o % span * sets + o // span), 0) if edges <= 128 else (ROWS * part * o, 0)
        row, lane = lane // 128, lane % 128
        for j in range(per):
            rows2[pl.ds(per * o + j, len(mids), stride=per * KEPT), :] = pltpu.roll(
                recv2[:, j, row, :], (128 - lane) % 128, 1
            ) if lane else recv2[:, j, row, :]
    back = [rows2[pl.ds(128 * i, 128), :].T for i in range(ep // 128)]
    back = jnp.concatenate(back, axis=1) if len(back) > 1 else back[0]
    comp = []
    for t in range(7):
        block = back[8 * (t // 2) : 8 * (t // 2) + 8]
        comp.append(pltpu.roll(block, 4, 0) if t % 2 else block)
    for t in range(6):
        pose_ref[t : t + 1, :] = comp[t][1:2, :edges]
    relative = exp_rotation(comp[:3])
    second = step(base, link, relative, comp[6], everyone)
    link = between(second, (1,), -1)
    final = step(second, link, relative, comp[6], (1,))
    for c in range(9):
        rot_ref[c : c + 1, :] = final[c][1:2]

    @pl.when(is_mid)
    def _():
        sent = send1.at[pl.ds(0, n - KEPT)]
        pltpu.make_async_copy(sent, sent, s1).wait()
        sent = send2.at[pl.ds(0, n - 1)]
        pltpu.make_async_copy(sent, sent, s2).wait()

    @pl.when(jnp.logical_not(is_mid))
    def _():
        pltpu.make_async_copy(send1, send1, s1).wait()

    pltpu.make_async_copy(rvh.at[pl.ds(0, 4)], rvh.at[pl.ds(0, 4)], hs).wait()
    pltpu.make_async_copy(sch.at[pl.ds(0, 2)], sch.at[pl.ds(0, 2)], es).wait()
    pltpu.make_async_copy(nbh.at[pl.ds(0, 2)], nbh.at[pl.ds(0, 2)], ns).wait()


def finish(pose_ref, rot_ref, pose_out, rot_out, sems):
    copies = [
        pltpu.make_async_copy(pose_ref, pose_out, sems.at[0]),
        pltpu.make_async_copy(rot_ref, rot_out, sems.at[1]),
    ]
    for copy in copies:
        copy.start()
    for copy in copies:
        copy.wait()


def solution(mesh):
    regions, pairs = mesh.shape["region"], mesh.shape["pair"]
    n = regions * pairs

    def on_device(points, offsets, normals, block_count, block_edge, edge_scan, edge_nbr, rotvec):
        blocks, edges, scans = points.shape[1], edge_scan.shape[0], rotvec.shape[1]
        slot, per = blocks // n, edges // n
        m1 = slot * ROWS // 128
        ep = max(edges, 128)
        sets = KEPT * edges // 128
        lines = max(edges // 128, 1)
        dma = pltpu.SemaphoreType.DMA
        vm = pl.BlockSpec(memory_space=pltpu.VMEM)
        hbm = pl.BlockSpec(memory_space=pl.ANY)
        pose, rot = pl.pallas_call(
            functools.partial(kernel, (regions, pairs, blocks, edges, scans)),
            out_shape=(pltpu.VMEM((6, edges), F32), pltpu.VMEM((9, scans), F32)),
            in_specs=[hbm] * 8,
            out_specs=(vm, vm),
            scratch_shapes=[
                pltpu.VMEM((blocks // 128, 3, 3, 128, 128), F32),
                pltpu.VMEM((9, 128, 128), F32),
                pltpu.VMEM((128, 128), F32),
                pltpu.VMEM((max(blocks, KEPT * edges), 128), F32),
                pltpu.VMEM((n, m1, 128), F32),
                pltpu.VMEM((n, KEPT, m1, 128), F32),
                pltpu.VMEM((8 * ROWS, 128), F32),
                pltpu.VMEM((3, 8 * sets, 128), F32),
                pltpu.VMEM((sets, ROWS, 128), F32),
                pltpu.VMEM((n, per, lines, 128), F32),
                pltpu.VMEM((n // KEPT, per, lines, 128), F32),
                pltpu.VMEM((ep, 128), F32),
                pltpu.VMEM((8, 3, scans), F32),
                pltpu.VMEM((3, 1, edges), jnp.int32),
                pltpu.VMEM((3, 1, edges), jnp.int32),
                pltpu.VMEM((3 * scans, 3 * ep), BF16),
                pltpu.VMEM((scans, 3 * ep), BF16),
                pltpu.VMEM((1, blocks), jnp.int32),
                pltpu.VMEM((1, blocks), jnp.int32),
                dma((blocks // 128, 3)),
                dma((2,)),
                dma, dma, dma, dma, dma, dma, dma, dma, dma, dma,
            ],
            compiler_params=pltpu.CompilerParams(collective_id=0, has_side_effects=True),
        )(
            points, offsets, normals, block_count[None], block_edge[None],
            edge_scan[None], edge_nbr[None], rotvec,
        )
        return pl.pallas_call(
            finish,
            out_shape=(
                jax.ShapeDtypeStruct((6, edges), F32),
                jax.ShapeDtypeStruct((9, scans), F32),
            ),
            in_specs=[vm] * 2,
            out_specs=(hbm, hbm),
            scratch_shapes=[dma((2,))],
        )(*(pltpu.with_memory_space_constraint(x, pltpu.VMEM) for x in (pose, rot)))

    flat = P(("region", "pair"))
    cut = P(None, ("region", "pair"))
    return jax.shard_map(
        on_device,
        mesh=mesh,
        in_specs=(P(None, ("region", "pair"), None),) * 3 + (flat,) * 4 + (cut,),
        out_specs=(cut, cut),
        check_vma=False,
    )
```

```python
import functools
import math

import jax
import jax.numpy as jnp
from jax import lax
from jax.experimental import pallas as pl
from jax.experimental.pallas import tpu as pltpu
from jax.sharding import PartitionSpec as P

damping = 16.0
min_length = 0.1
MESH = pl.DeviceIdType.MESH
F32 = jnp.float32
BF16 = jnp.bfloat16
ROWS = 32
KEPT = 4


def owners(regions, pairs):
    near = sorted(
        ((r, p) for r in range(regions) for p in range(pairs)),
        key=lambda at: (at[0] // 2 + at[1] // 2 + at[1] % 2, at[0] // 2, at[1], at[0]),
    )
    return sorted(near[: regions * pairs // KEPT])


def exp_rotation(v):
    t = v[0] * v[0] + v[1] * v[1] + v[2] * v[2]
    a = 1.0 + t * (-1.0 / 6.0 + t * (1.0 / 120.0 + t * (-1.0 / 5040.0 + t * (1.0 / 362880.0))))
    b = 0.5 + t * (-1.0 / 24.0 + t * (1.0 / 720.0 + t * (-1.0 / 40320.0 + t * (1.0 / 3628800.0))))
    bv = [b * v[i] for i in range(3)]
    av = [a * v[i] for i in range(3)]
    diag = 1.0 - b * t
    xy, xz, yz = bv[0] * v[1], bv[0] * v[2], bv[1] * v[2]
    return [
        diag + bv[0] * v[0], xy - av[2], xz + av[1],
        xy + av[2], diag + bv[1] * v[1], yz - av[0],
        xz - av[1], yz + av[0], diag + bv[2] * v[2],
    ]


def angle(s, c):
    size = jnp.abs(c)
    big, small = jnp.maximum(s, size), jnp.minimum(s, size)
    far = small > 0.41421356 * big
    z = jnp.where(far, small - big, small) / jnp.maximum(jnp.where(far, small + big, big), 1e-30)
    z2 = z * z
    poly = ((8.05374449538e-2 * z2 - 1.38776856032e-1) * z2 + 1.99777106478e-1) * z2 - 3.33329491539e-1
    r = jnp.where(far, math.pi / 4, 0.0) + (z + z * z2 * poly)
    r = jnp.where(s > size, math.pi / 2 - r, r)
    return jnp.where(c < 0.0, math.pi - r, r)


def log_rotation(m):
    c = (m[0] + m[4] + m[8] - 1.0) * 0.5
    u = [0.5 * (m[7] - m[5]), 0.5 * (m[2] - m[6]), 0.5 * (m[3] - m[1])]
    s2 = u[0] * u[0] + u[1] * u[1] + u[2] * u[2]
    s = jnp.sqrt(s2)
    f = jnp.where(s < 0.0001, 1.0 + s2 / 6.0, angle(s, c) / jnp.maximum(s, 0.0001))
    return [f * x for x in u]


def mat_mul(x, y):
    return [sum(x[3 * a + b] * y[3 * b + c] for b in range(3)) for a in range(3) for c in range(3)]


def mat_tmul(x, y):
    return [sum(x[3 * b + a] * y[3 * b + c] for b in range(3)) for a in range(3) for c in range(3)]


def split_pair(x):
    hi = x.astype(BF16)
    mid = (x - hi.astype(F32)).astype(BF16)
    return jnp.concatenate([hi, mid], axis=0)


def exact_dot(x, table, dims):
    rows = x.shape[0]
    out = lax.dot_general(split_pair(x), table, (dims, ((), ())), preferred_element_type=F32)
    return out[:rows] + out[rows:]


def one_hot(index, count, width):
    grid = lax.broadcasted_iota(jnp.int32, (count, width), 0)
    return jnp.where(grid == index, 1.0, 0.0).astype(BF16)


def solve(h, g):
    low = [[None] * 6 for _ in range(6)]
    val = [[None] * 6 for _ in range(6)]
    inv = [None] * 6
    for c in range(6):
        for r in range(c, 6):
            x = h[r][c]
            for k in range(c):
                x = x - val[r][k] * low[c][k]
            val[r][c] = x
        inv[c] = 1.0 / val[c][c]
        for r in range(c + 1, 6):
            low[r][c] = val[r][c] * inv[c]
    y = []
    for r in range(6):
        x = g[r]
        for k in range(r):
            x = x - low[r][k] * y[k]
        y.append(x)
    out = [None] * 6
    for r in range(5, -1, -1):
        x = y[r] * inv[r]
        for k in range(r + 1, 6):
            x = x - low[k][r] * out[k]
        out[r] = x
    return out


def kernel(
    sizes,
    pts_hbm, off_hbm, nrm_hbm, cnt_hbm, edge_hbm, scan_ref, nbr_ref, rv_ref,
    pose_ref, rot_ref,
    data, tr, tt, tab, send1, recv1, sums_ref, poses, groups, send2, recv2, rows2,
    rvh, sch, nbh, near_tab, own_tab, cnt_ref, edge_ref,
    in_sem, int_sem, s1, r1, s2, r2, hs, hr, es, er, ns, nr,
):
    regions, pairs, blocks, edges, scans = sizes
    n = regions * pairs
    slot = blocks // n
    per = edges // n
    per_row = 128 // ROWS
    m1 = slot * ROWS // 128
    ep = max(edges, 128)
    halves = blocks // 128
    reg, pair = lax.axis_index("region"), lax.axis_index("pair")
    me = reg * pairs + pair

    def wrapped(x, size):
        return jnp.where(x >= size, x - size, x)

    mids = owners(regions, pairs)

    def holds(r, p):
        hit = [jnp.logical_and(r == a, p == b) for a, b in mids]
        return functools.reduce(jnp.logical_or, hit)

    is_mid = holds(reg, pair)
    rank = sum(jnp.where(me == r * pairs + p, k, 0) for k, (r, p) in enumerate(mids))
    beside = sorted({k % regions for k in (-2, -1, 1, 2)})

    def each_mid(send):
        @pl.when(is_mid)
        def _():
            for k, where in enumerate(mids):
                @pl.when(rank != k)
                def _():
                    send(k, where)

        @pl.when(jnp.logical_not(is_mid))
        def _():
            for k, where in enumerate(mids):
                send(k, where)

    def each_other(send):
        def step(dp, carry):
            p = wrapped(pair + pairs - dp, pairs)
            for dr in range(regions):
                r = wrapped(reg + dr, regions)
                send(r * pairs + p, (r, p))
            return carry

        for dr in range(1, regions):
            r = wrapped(reg + dr, regions)
            send(r * pairs + pair, (r, pair))
        lax.fori_loop(1, pairs, step, 0)

    ints = [
        pltpu.make_async_copy(cnt_hbm, cnt_ref, int_sem.at[0]),
        pltpu.make_async_copy(edge_hbm, edge_ref, int_sem.at[1]),
    ]
    for copy in ints:
        copy.start()
    loads = []
    for h in range(halves):
        for a, ref in enumerate((pts_hbm, off_hbm, nrm_hbm)):
            copy = pltpu.make_async_copy(
                ref.at[:, pl.ds(h * 128, 128), :], data.at[h, a], in_sem.at[h, a]
            )
            copy.start()
            loads.append(copy)

    barrier = pltpu.get_barrier_semaphore()


    def greet(to, where):
        pl.semaphore_signal(barrier, inc=1, device_id=where, device_id_type=MESH)

    sides = [wrapped(reg + dr, regions) for dr in beside]
    apart = [jnp.logical_not(holds(r, pair)) for r in sides]

    @pl.when(is_mid)
    def _():
        each_other(greet)

    @pl.when(jnp.logical_not(is_mid))
    def _():
        for r, p in mids:
            greet(r * pairs + p, (r, p))
        for r, other in zip(sides, apart):
            @pl.when(other)
            def _():
                greet(r, (r, pair))

    groups[...] = jnp.zeros_like(groups)
    poses[...] = jnp.zeros_like(poses)
    sums_ref[...] = jnp.zeros_like(sums_ref)
    tt[pl.ds(8 * 27, 8 * 5), :] = jnp.zeros((8 * 5, 128), F32)
    rvh[pl.ds(5, 3)] = jnp.zeros((3, 3, scans), F32)
    rows2[...] = jnp.zeros_like(rows2)
    for copy in ints:
        copy.wait()
    def turn(h, i):
        tr[h % 2, i] = data[h, i // 3, i % 3].T

    def chunk(h, at, acc):
        p = [tr[h % 2, c, pl.ds(at, 8), :] for c in range(3)]
        d = [tr[h % 2, 3 + c, pl.ds(at, 8), :] for c in range(3)]
        live = lax.broadcasted_iota(jnp.int32, (8, 128), 0) + at < cnt_ref[:, h * 128 : (h + 1) * 128]
        v = [jnp.where(live, tr[h % 2, 6 + c, pl.ds(at, 8), :], 0.0) for c in range(3)]
        jac = [
            p[1] * v[2] - p[2] * v[1],
            p[2] * v[0] - p[0] * v[2],
            p[0] * v[1] - p[1] * v[0],
        ] + v
        resid = v[0] * d[0] + v[1] * d[1] + v[2] * d[2]
        new = [jac[x] * jac[y] for x in range(6) for y in range(x + 1)] + [x * resid for x in jac]
        return [a + b for a, b in zip(acc, new)] if acc else new

    for a in range(3):
        loads[a].wait()
        for c in range(3):
            turn(0, 3 * a + c)
    for h in range(halves):
        more = h + 1 < halves
        if more:
            for a in range(3):
                loads[3 * h + 3 + a].wait()
        acc, done = [], 0
        for i in range(16):
            acc = chunk(h, 8 * i, acc)
            while more and done * 16 < 9 * (i + 1):
                turn(h + 1, done)
                done += 1
        for t in range(27):
            tt[8 * t : 8 * t + 8, :] = acc[t]
        tt[8 * 27 : 8 * 27 + 1, :] = jnp.where(cnt_ref[:, h * 128 : (h + 1) * 128] > 0, 1.0, 0.0)
        tt[8 * 28 : 8 * 28 + 1, :] = edge_ref[:, h * 128 : (h + 1) * 128].astype(F32)
        total = [tt[pl.ds(u, ROWS, stride=8), :] for u in range(8)]
        while len(total) > 1:
            total = [x + y for x, y in zip(total[::2], total[1::2])]
        tab[pl.ds(h * 128, 128), :ROWS] = total[0].T
    lane = lax.broadcasted_iota(jnp.int32, (n, 128), 1)
    for j in range(m1):
        row = tab[pl.ds(j * per_row, n, stride=slot), :]
        for k in range(1, per_row):
            moved = pltpu.roll(tab[pl.ds(j * per_row + k, n, stride=slot), :], ROWS * k, 1)
            row = jnp.where(lane < ROWS * k, row, moved)
        send1[:, j, :] = row

    @pl.when(is_mid)
    def _():
        pl.semaphore_wait(barrier, n - 1)

    @pl.when(jnp.logical_not(is_mid))
    def _():
        pl.semaphore_wait(barrier, len(mids) + sum(other.astype(jnp.int32) for other in apart))

    each_mid(
        lambda k, where: pltpu.make_async_remote_copy(
            send1.at[pl.ds(k * KEPT, KEPT)], recv1.at[me], s1, r1, device_id=where, device_id_type=MESH
        ).start()
    )

    @pl.when(is_mid)
    def _():
        pltpu.make_async_copy(send1.at[pl.ds(rank * KEPT, KEPT)], recv1.at[me], r1).start()

    for k in (-1, 1, -2, 2):
        where = (wrapped(reg + k % regions, regions), pair)
        pltpu.make_async_remote_copy(
            rv_ref, rvh.at[2 - k], hs, hr, device_id=where, device_id_type=MESH
        ).start()
        if abs(k) == 1:
            pltpu.make_async_remote_copy(
                scan_ref, sch.at[1 - k], es, er, device_id=where, device_id_type=MESH
            ).start()
            pltpu.make_async_remote_copy(
                nbr_ref, nbh.at[1 - k], ns, nr, device_id=where, device_id_type=MESH
            ).start()
    pltpu.make_async_copy(rv_ref, rvh.at[2], hr).start()
    pltpu.make_async_copy(scan_ref, sch.at[1], er).start()
    pltpu.make_async_copy(nbr_ref, nbh.at[1], nr).start()

    @pl.when(is_mid)
    def _():
        pltpu.make_async_copy(recv1, recv1, r1).wait()
        wide = max(edges, 128)
        span = wide // edges
        lanes = m1 * n
        for q in range(KEPT // span):
            got = [recv1[:, q * span + h, j, :] for h in range(span) for j in range(m1)]
            got = jnp.concatenate(got, axis=0)
            turned_rows = [got[128 * i : 128 * (i + 1)].T for i in range(span * lanes // 128)]
            turned_rows = jnp.concatenate(turned_rows, axis=1) if len(turned_rows) > 1 else turned_rows[0]
            mine = [turned_rows[ROWS * k : ROWS * (k + 1)] for k in range(per_row)]
            owner = lax.broadcasted_iota(jnp.int32, (1, span * lanes), 1) // lanes * edges
            offset = owner.astype(F32)
            slots = lax.broadcasted_iota(jnp.int32, (wide, span * lanes), 0).astype(F32)
            table = [jnp.where(slots == x[28:29] + offset, 1.0, 0.0).astype(BF16) for x in mine]
            total = exact_dot(
                jnp.concatenate(mine, axis=1), jnp.concatenate(table, axis=1), ((1,), (1,))
            )
            for i in range(wide // 128):
                sums_ref[pl.ds(q * (wide // 128) + i, ROWS, stride=8), :] = total[:, 128 * i : 128 * (i + 1)]
        sets = KEPT * edges // 128
        h, at_t = [[None] * 6 for _ in range(6)], 0
        for x in range(6):
            for y in range(x + 1):
                h[x][y] = sums_ref[8 * at_t : 8 * at_t + 8, :] + (damping if x == y else 0.0)
                at_t += 1
        pose = [-x for x in solve(h, [sums_ref[8 * (21 + x) : 8 * (22 + x), :] for x in range(6)])]
        payload = pose + [jnp.where(sums_ref[8 * 27 : 8 * 28, :] > 0.5, 1.0, 0.0)]
        for t in range(7):
            poses[1, sets * t : sets * (t + 1), :] = payload[t][:sets]
        stacked = poses[1]

        def turned(x, by):
            if edges <= 128:
                lane = lax.rem(lax.broadcasted_iota(jnp.int32, x.shape, 1), edges)
                one = pltpu.roll(x, by, 1)
                two = pltpu.roll(x, (by - edges) % 128, 1)
                return jnp.where(lane < by, two, one)
            part = edges // 128
            row = lax.rem(lax.broadcasted_iota(jnp.int32, x.shape, 0), part)
            tall = x.shape[0]

            def moved(k):
                back = k % part
                if back == 0:
                    return x
                return jnp.where(
                    row >= back, pltpu.roll(x, back, 0), pltpu.roll(x, (back - part) % tall, 0)
                )

            lane = lax.broadcasted_iota(jnp.int32, x.shape, 1)
            whole, rest = by // 128, by % 128
            if rest == 0:
                return moved(whole)
            return jnp.where(
                lane < rest, pltpu.roll(moved(whole + 1), rest, 1), pltpu.roll(moved(whole), rest, 1)
            )

        poses[0] = turned(stacked, per * pairs)
        poses[2] = turned(stacked, edges - per * pairs)
        for q in range(sets):
            for g in range(3):
                groups[q, pl.ds(g, 8, stride=4), :] = poses[g, pl.ds(q, 8, stride=sets), :]
        held = 128 // ROWS
        for q in range(0, sets, held):
            some = range(q, min(q + held, sets))
            flat = jnp.concatenate([groups[i] for i in some], axis=0)
            if len(some) < held:
                flat = jnp.concatenate([flat, jnp.zeros((128 - ROWS * len(some), 128), F32)], axis=0)
            tab[pl.ds(128 * (q // held), 128), :] = flat.T
        for j in range(per):
            if edges <= 128:
                row = tab[pl.ds(j, n, stride=per), :]
                for h2 in range(1, span):
                    row = row + pltpu.roll(tab[pl.ds(h2 * edges + j, n, stride=per), :], ROWS * sets * h2, 1)
                send2[:, j, 0, :] = row
            else:
                part = edges // 128
                count = 128 // per
                for i in range(sets // held):
                    block = tab[pl.ds(128 * i + j, count, stride=per), :]
                    for b in range(part):
                        send2[pl.ds(b * count, count), j, i, :] = pltpu.roll(block, (128 - ROWS * b) % 128, 1)
        each_other(
            lambda to, where: pltpu.make_async_remote_copy(
                send2.at[to], recv2.at[rank], s2, r2, device_id=where, device_id_type=MESH
            ).start()
        )
        pltpu.make_async_copy(send2.at[me], recv2.at[rank], r2).start()

    pltpu.make_async_copy(rvh.at[pl.ds(0, 5)], rvh.at[pl.ds(0, 5)], hr).wait()
    pltpu.make_async_copy(sch, sch, er).wait()
    pltpu.make_async_copy(nbh, nbh, nr).wait()
    for q in range(3):
        near_tab[:, q * ep : q * ep + edges] = one_hot(nbh[q], 3 * scans, edges)
        own_tab[:, q * ep : q * ep + edges] = one_hot(sch[q], scans, edges)
        if ep > edges:
            near_tab[:, q * ep + edges : (q + 1) * ep] = jnp.zeros((3 * scans, ep - edges), BF16)
            own_tab[:, q * ep + edges : (q + 1) * ep] = jnp.zeros((scans, ep - edges), BF16)

    def up(x, k):
        return pltpu.roll(x, (8 - k) % 8, 0) if k % 8 else x

    def picked(out, c, sets, width):
        block = out[8 * c : 8 * c + 8]
        if len(sets) == 1:
            return block
        value = block[:, :width]
        for q in sets[1:]:
            value = jnp.where(
                lax.broadcasted_iota(jnp.int32, (8, width), 0) == q,
                block[:, q * width : (q + 1) * width],
                value,
            )
        return value

    def between(rot, sets, shift):
        cols = pl.ds(sets[0] * ep, len(sets) * ep)
        parts = [
            jnp.concatenate([up(x, s + shift) for x in rot], axis=0) for s in range(3)
        ]
        near = exact_dot(jnp.concatenate(parts, axis=1), near_tab[:, cols], ((1,), (0,)))
        mine = exact_dot(parts[1], own_tab[:, cols], ((1,), (0,)))
        return mat_tmul(
            [picked(mine, c, sets, ep) for c in range(9)],
            [picked(near, c, sets, ep) for c in range(9)],
        )

    def step(rot, link, relative, live, sets):
        cols = pl.ds(sets[0] * ep, len(sets) * ep)
        tangent = log_rotation(mat_mul(link, relative))
        length = jnp.sqrt(tangent[0] * tangent[0] + tangent[1] * tangent[1] + tangent[2] * tangent[2])
        weight = live / jnp.maximum(length, min_length)
        weighed = jnp.concatenate([weight * x for x in tangent] + [weight], axis=0)
        parts = [
            exact_dot(weighed, own_tab[:, pl.ds(q * ep, ep)], ((1,), (1,))) for q in sets
        ]
        total = jnp.concatenate(parts, axis=1)
        numer = [picked(total, c, sets, scans) for c in range(3)]
        scale = 1.0 / (picked(total, 3, sets, scans) + 1.0)
        return mat_mul(rot, exp_rotation([x * scale for x in numer]))

    first = exp_rotation([rvh[:, c, :] for c in range(3)])
    everyone = (0, 1, 2)
    link = between(first, everyone, 0)
    base = [up(x, 1) for x in first]

    pltpu.make_async_copy(recv2, recv2, r2).wait()
    part = max(edges // 128, 1)
    span = max(128 // edges, 1)
    sets = KEPT * edges // 128
    for o in range(KEPT):
        lane, row = (ROWS * (o % span * sets + o // span), 0) if edges <= 128 else (ROWS * part * o, 0)
        row, lane = lane // 128, lane % 128
        for j in range(per):
            rows2[pl.ds(per * o + j, len(mids), stride=per * KEPT), :] = pltpu.roll(
                recv2[:, j, row, :], (128 - lane) % 128, 1
            ) if lane else recv2[:, j, row, :]
    back = [rows2[pl.ds(128 * i, 128), :].T for i in range(ep // 128)]
    back = jnp.concatenate(back, axis=1) if len(back) > 1 else back[0]
    comp = []
    for t in range(7):
        block = back[8 * (t // 2) : 8 * (t // 2) + 8]
        comp.append(pltpu.roll(block, 4, 0) if t % 2 else block)
    for t in range(6):
        pose_ref[t : t + 1, :] = comp[t][1:2, :edges]
    relative = exp_rotation(comp[:3])
    second = step(base, link, relative, comp[6], everyone)
    link = between(second, (1,), -1)
    final = step(second, link, relative, comp[6], (1,))
    for c in range(9):
        rot_ref[c : c + 1, :] = final[c][1:2]

    @pl.when(is_mid)
    def _():
        sent = send1.at[pl.ds(0, n - KEPT)]
        pltpu.make_async_copy(sent, sent, s1).wait()
        sent = send2.at[pl.ds(0, n - 1)]
        pltpu.make_async_copy(sent, sent, s2).wait()

    @pl.when(jnp.logical_not(is_mid))
    def _():
        pltpu.make_async_copy(send1, send1, s1).wait()

    pltpu.make_async_copy(rvh.at[pl.ds(0, 4)], rvh.at[pl.ds(0, 4)], hs).wait()
    pltpu.make_async_copy(sch.at[pl.ds(0, 2)], sch.at[pl.ds(0, 2)], es).wait()
    pltpu.make_async_copy(nbh.at[pl.ds(0, 2)], nbh.at[pl.ds(0, 2)], ns).wait()


def finish(pose_ref, rot_ref, pose_out, rot_out, sems):
    copies = [
        pltpu.make_async_copy(pose_ref, pose_out, sems.at[0]),
        pltpu.make_async_copy(rot_ref, rot_out, sems.at[1]),
    ]
    for copy in copies:
        copy.start()
    for copy in copies:
        copy.wait()


def solution(mesh):
    regions, pairs = mesh.shape["region"], mesh.shape["pair"]
    n = regions * pairs

    def on_device(points, offsets, normals, block_count, block_edge, edge_scan, edge_nbr, rotvec):
        blocks, edges, scans = points.shape[1], edge_scan.shape[0], rotvec.shape[1]
        slot, per = blocks // n, edges // n
        m1 = slot * ROWS // 128
        ep = max(edges, 128)
        sets = KEPT * edges // 128
        lines = max(edges // 128, 1)
        dma = pltpu.SemaphoreType.DMA
        vm = pl.BlockSpec(memory_space=pltpu.VMEM)
        hbm = pl.BlockSpec(memory_space=pl.ANY)
        pose, rot = pl.pallas_call(
            functools.partial(kernel, (regions, pairs, blocks, edges, scans)),
            out_shape=(pltpu.VMEM((6, edges), F32), pltpu.VMEM((9, scans), F32)),
            in_specs=[hbm] * 8,
            out_specs=(vm, vm),
            scratch_shapes=[
                pltpu.VMEM((blocks // 128, 3, 3, 128, 128), F32),
                pltpu.VMEM((2, 9, 128, 128), F32),
                pltpu.VMEM((8 * ROWS, 128), F32),
                pltpu.VMEM((max(blocks, KEPT * edges), 128), F32),
                pltpu.VMEM((n, m1, 128), F32),
                pltpu.VMEM((n, KEPT, m1, 128), F32),
                pltpu.VMEM((8 * ROWS, 128), F32),
                pltpu.VMEM((3, 8 * sets, 128), F32),
                pltpu.VMEM((sets, ROWS, 128), F32),
                pltpu.VMEM((n, per, lines, 128), F32),
                pltpu.VMEM((n // KEPT, per, lines, 128), F32),
                pltpu.VMEM((ep, 128), F32),
                pltpu.VMEM((8, 3, scans), F32),
                pltpu.VMEM((3, 1, edges), jnp.int32),
                pltpu.VMEM((3, 1, edges), jnp.int32),
                pltpu.VMEM((3 * scans, 3 * ep), BF16),
                pltpu.VMEM((scans, 3 * ep), BF16),
                pltpu.VMEM((1, blocks), jnp.int32),
                pltpu.VMEM((1, blocks), jnp.int32),
                dma((blocks // 128, 3)),
                dma((2,)),
                dma, dma, dma, dma, dma, dma, dma, dma, dma, dma,
            ],
            compiler_params=pltpu.CompilerParams(collective_id=0, has_side_effects=True),
        )(
            points, offsets, normals, block_count[None], block_edge[None],
            edge_scan[None], edge_nbr[None], rotvec,
        )
        return pl.pallas_call(
            finish,
            out_shape=(
                jax.ShapeDtypeStruct((6, edges), F32),
                jax.ShapeDtypeStruct((9, scans), F32),
            ),
            in_specs=[vm] * 2,
            out_specs=(hbm, hbm),
            scratch_shapes=[dma((2,))],
        )(*(pltpu.with_memory_space_constraint(x, pltpu.VMEM) for x in (pose, rot)))

    flat = P(("region", "pair"))
    cut = P(None, ("region", "pair"))
    return jax.shard_map(
        on_device,
        mesh=mesh,
        in_specs=(P(None, ("region", "pair"), None),) * 3 + (flat,) * 4 + (cut,),
        out_specs=(cut, cut),
        check_vma=False,
    )
```

```python
import functools
import math

import jax
import jax.numpy as jnp
from jax import lax
from jax.experimental import pallas as pl
from jax.experimental.pallas import tpu as pltpu
from jax.sharding import PartitionSpec as P

damping = 16.0
min_length = 0.1
MESH = pl.DeviceIdType.MESH
F32 = jnp.float32
BF16 = jnp.bfloat16
ROWS = 32
KEPT = 4


def owners(regions, pairs):
    near = sorted(
        ((r, p) for r in range(regions) for p in range(pairs)),
        key=lambda at: (at[0] // 2 + at[1] // 2 + at[1] % 2, at[0] // 2, at[1], at[0]),
    )
    return sorted(near[: regions * pairs // KEPT])


def exp_rotation(v):
    t = v[0] * v[0] + v[1] * v[1] + v[2] * v[2]
    a = 1.0 + t * (-1.0 / 6.0 + t * (1.0 / 120.0 + t * (-1.0 / 5040.0 + t * (1.0 / 362880.0))))
    b = 0.5 + t * (-1.0 / 24.0 + t * (1.0 / 720.0 + t * (-1.0 / 40320.0 + t * (1.0 / 3628800.0))))
    bv = [b * v[i] for i in range(3)]
    av = [a * v[i] for i in range(3)]
    diag = 1.0 - b * t
    xy, xz, yz = bv[0] * v[1], bv[0] * v[2], bv[1] * v[2]
    return [
        diag + bv[0] * v[0], xy - av[2], xz + av[1],
        xy + av[2], diag + bv[1] * v[1], yz - av[0],
        xz - av[1], yz + av[0], diag + bv[2] * v[2],
    ]


def angle(s, c):
    size = jnp.abs(c)
    big, small = jnp.maximum(s, size), jnp.minimum(s, size)
    far = small > 0.41421356 * big
    z = jnp.where(far, small - big, small) / jnp.maximum(jnp.where(far, small + big, big), 1e-30)
    z2 = z * z
    poly = ((8.05374449538e-2 * z2 - 1.38776856032e-1) * z2 + 1.99777106478e-1) * z2 - 3.33329491539e-1
    r = jnp.where(far, math.pi / 4, 0.0) + (z + z * z2 * poly)
    r = jnp.where(s > size, math.pi / 2 - r, r)
    return jnp.where(c < 0.0, math.pi - r, r)


def log_rotation(m):
    c = (m[0] + m[4] + m[8] - 1.0) * 0.5
    u = [0.5 * (m[7] - m[5]), 0.5 * (m[2] - m[6]), 0.5 * (m[3] - m[1])]
    s2 = u[0] * u[0] + u[1] * u[1] + u[2] * u[2]
    s = jnp.sqrt(s2)
    f = jnp.where(s < 0.0001, 1.0 + s2 / 6.0, angle(s, c) / jnp.maximum(s, 0.0001))
    return [f * x for x in u]


def mat_mul(x, y):
    return [sum(x[3 * a + b] * y[3 * b + c] for b in range(3)) for a in range(3) for c in range(3)]


def mat_tmul(x, y):
    return [sum(x[3 * b + a] * y[3 * b + c] for b in range(3)) for a in range(3) for c in range(3)]


def split_pair(x):
    hi = x.astype(BF16)
    mid = (x - hi.astype(F32)).astype(BF16)
    return jnp.concatenate([hi, mid], axis=0)


def exact_dot(x, table, dims):
    rows = x.shape[0]
    out = lax.dot_general(split_pair(x), table, (dims, ((), ())), preferred_element_type=F32)
    return out[:rows] + out[rows:]


def one_hot(index, count, width):
    grid = lax.broadcasted_iota(jnp.int32, (count, width), 0)
    return jnp.where(grid == index, 1.0, 0.0).astype(BF16)


def solve(h, g):
    low = [[None] * 6 for _ in range(6)]
    val = [[None] * 6 for _ in range(6)]
    inv = [None] * 6
    for c in range(6):
        for r in range(c, 6):
            x = h[r][c]
            for k in range(c):
                x = x - val[r][k] * low[c][k]
            val[r][c] = x
        inv[c] = 1.0 / val[c][c]
        for r in range(c + 1, 6):
            low[r][c] = val[r][c] * inv[c]
    y = []
    for r in range(6):
        x = g[r]
        for k in range(r):
            x = x - low[r][k] * y[k]
        y.append(x)
    out = [None] * 6
    for r in range(5, -1, -1):
        x = y[r] * inv[r]
        for k in range(r + 1, 6):
            x = x - low[k][r] * out[k]
        out[r] = x
    return out


def kernel(
    sizes,
    pts_hbm, off_hbm, nrm_hbm, cnt_hbm, edge_hbm, scan_ref, nbr_ref, rv_ref,
    pose_ref, rot_ref,
    data, tr, tt, tab, send1, recv1, sums_ref, poses, groups, send2, recv2, rows2,
    rvh, sch, nbh, near_tab, own_tab, cnt_ref, edge_ref,
    in_sem, int_sem, s1, r1, s2, r2, hs, hr, es, er, ns, nr,
):
    regions, pairs, blocks, edges, scans = sizes
    n = regions * pairs
    slot = blocks // n
    per = edges // n
    per_row = 128 // ROWS
    m1 = slot * ROWS // 128
    block = KEPT * m1
    ep = max(edges, 128)
    halves = blocks // 128
    reg, pair = lax.axis_index("region"), lax.axis_index("pair")
    me = reg * pairs + pair

    def wrapped(x, size):
        return jnp.where(x >= size, x - size, x)

    mids = owners(regions, pairs)

    def holds(r, p):
        hit = [jnp.logical_and(r == a, p == b) for a, b in mids]
        return functools.reduce(jnp.logical_or, hit)

    is_mid = holds(reg, pair)
    rank = sum(jnp.where(me == r * pairs + p, k, 0) for k, (r, p) in enumerate(mids))
    beside = sorted({k % regions for k in (-2, -1, 1, 2)})

    def each_mid(send):
        @pl.when(is_mid)
        def _():
            for k, where in enumerate(mids):
                @pl.when(rank != k)
                def _():
                    send(k, where)

        @pl.when(jnp.logical_not(is_mid))
        def _():
            for k, where in enumerate(mids):
                send(k, where)

    def each_other(send):
        def step(dp, carry):
            p = wrapped(pair + pairs - dp, pairs)
            for dr in range(regions):
                r = wrapped(reg + dr, regions)
                send(r * pairs + p, (r, p))
            return carry

        for dr in range(1, regions):
            r = wrapped(reg + dr, regions)
            send(r * pairs + pair, (r, pair))
        lax.fori_loop(1, pairs, step, 0)

    ints = [
        pltpu.make_async_copy(cnt_hbm, cnt_ref, int_sem.at[0]),
        pltpu.make_async_copy(edge_hbm, edge_ref, int_sem.at[1]),
    ]
    for copy in ints:
        copy.start()
    loads = []
    for h in range(halves):
        for a, ref in enumerate((pts_hbm, off_hbm, nrm_hbm)):
            copy = pltpu.make_async_copy(
                ref.at[:, pl.ds(h * 128, 128), :], data.at[h, a], in_sem.at[h, a]
            )
            copy.start()
            loads.append(copy)

    barrier = pltpu.get_barrier_semaphore()


    def greet(to, where):
        pl.semaphore_signal(barrier, inc=1, device_id=where, device_id_type=MESH)

    sides = [wrapped(reg + dr, regions) for dr in beside]
    apart = [jnp.logical_not(holds(r, pair)) for r in sides]

    @pl.when(is_mid)
    def _():
        each_other(greet)

    @pl.when(jnp.logical_not(is_mid))
    def _():
        for r, p in mids:
            greet(r * pairs + p, (r, p))
        for r, other in zip(sides, apart):
            @pl.when(other)
            def _():
                greet(r, (r, pair))

    groups[...] = jnp.zeros_like(groups)
    poses[...] = jnp.zeros_like(poses)
    sums_ref[...] = jnp.zeros_like(sums_ref)
    tt[pl.ds(8 * 27, 8 * 5), :] = jnp.zeros((8 * 5, 128), F32)
    rvh[pl.ds(5, 3)] = jnp.zeros((3, 3, scans), F32)
    rows2[...] = jnp.zeros_like(rows2)
    for copy in ints:
        copy.wait()
    def turn(h, i):
        tr[h % 2, i] = data[h, i // 3, i % 3].T

    def chunk(h, at, acc):
        p = [tr[h % 2, c, pl.ds(at, 8), :] for c in range(3)]
        d = [tr[h % 2, 3 + c, pl.ds(at, 8), :] for c in range(3)]
        live = lax.broadcasted_iota(jnp.int32, (8, 128), 0) + at < cnt_ref[:, h * 128 : (h + 1) * 128]
        v = [jnp.where(live, tr[h % 2, 6 + c, pl.ds(at, 8), :], 0.0) for c in range(3)]
        jac = [
            p[1] * v[2] - p[2] * v[1],
            p[2] * v[0] - p[0] * v[2],
            p[0] * v[1] - p[1] * v[0],
        ] + v
        resid = v[0] * d[0] + v[1] * d[1] + v[2] * d[2]
        new = [jac[x] * jac[y] for x in range(6) for y in range(x + 1)] + [x * resid for x in jac]
        return [a + b for a, b in zip(acc, new)] if acc else new

    for a in range(3):
        loads[a].wait()
        for c in range(3):
            turn(0, 3 * a + c)
    for h in range(halves):
        more = h + 1 < halves
        if more:
            for a in range(3):
                loads[3 * h + 3 + a].wait()
        acc, done = [], 0
        for i in range(16):
            acc = chunk(h, 8 * i, acc)
            while more and done * 16 < 9 * (i + 1):
                turn(h + 1, done)
                done += 1
        for t in range(27):
            tt[8 * t : 8 * t + 8, :] = acc[t]
        tt[8 * 27 : 8 * 27 + 1, :] = jnp.where(cnt_ref[:, h * 128 : (h + 1) * 128] > 0, 1.0, 0.0)
        tt[8 * 28 : 8 * 28 + 1, :] = edge_ref[:, h * 128 : (h + 1) * 128].astype(F32)
        total = [tt[pl.ds(u, ROWS, stride=8), :] for u in range(8)]
        while len(total) > 1:
            total = [x + y for x, y in zip(total[::2], total[1::2])]
        tab[pl.ds(h * 128, 128), :ROWS] = total[0].T
    lane = lax.broadcasted_iota(jnp.int32, (n, 128), 1)
    for j in range(m1):
        row = tab[pl.ds(j * per_row, n, stride=slot), :]
        for k in range(1, per_row):
            moved = pltpu.roll(tab[pl.ds(j * per_row + k, n, stride=slot), :], ROWS * k, 1)
            row = jnp.where(lane < ROWS * k, row, moved)
        send1[pl.ds(j, n, stride=m1), :] = row

    @pl.when(is_mid)
    def _():
        pl.semaphore_wait(barrier, n - 1)

    @pl.when(jnp.logical_not(is_mid))
    def _():
        pl.semaphore_wait(barrier, len(mids) + sum(other.astype(jnp.int32) for other in apart))

    each_mid(
        lambda k, where: pltpu.make_async_remote_copy(
            send1.at[pl.ds(k * block, block)], recv1.at[pl.ds(pl.multiple_of(me * block, block), block)], s1, r1, device_id=where, device_id_type=MESH
        ).start()
    )

    @pl.when(is_mid)
    def _():
        pltpu.make_async_copy(
            send1.at[pl.ds(pl.multiple_of(rank * block, block), block)],
            recv1.at[pl.ds(pl.multiple_of(me * block, block), block)], r1,
        ).start()

    for k in (-1, 1, -2, 2):
        where = (wrapped(reg + k % regions, regions), pair)
        pltpu.make_async_remote_copy(
            rv_ref, rvh.at[2 - k], hs, hr, device_id=where, device_id_type=MESH
        ).start()
        if abs(k) == 1:
            pltpu.make_async_remote_copy(
                scan_ref, sch.at[1 - k], es, er, device_id=where, device_id_type=MESH
            ).start()
            pltpu.make_async_remote_copy(
                nbr_ref, nbh.at[1 - k], ns, nr, device_id=where, device_id_type=MESH
            ).start()
    pltpu.make_async_copy(rv_ref, rvh.at[2], hr).start()
    pltpu.make_async_copy(scan_ref, sch.at[1], er).start()
    pltpu.make_async_copy(nbr_ref, nbh.at[1], nr).start()

    pltpu.make_async_copy(rvh.at[pl.ds(0, 5)], rvh.at[pl.ds(0, 5)], hr).wait()
    pltpu.make_async_copy(sch, sch, er).wait()
    pltpu.make_async_copy(nbh, nbh, nr).wait()
    for q in range(3):
        near_tab[:, q * ep : q * ep + edges] = one_hot(nbh[q], 3 * scans, edges)
        own_tab[:, q * ep : q * ep + edges] = one_hot(sch[q], scans, edges)
        if ep > edges:
            near_tab[:, q * ep + edges : (q + 1) * ep] = jnp.zeros((3 * scans, ep - edges), BF16)
            own_tab[:, q * ep + edges : (q + 1) * ep] = jnp.zeros((scans, ep - edges), BF16)

    def up(x, k):
        return pltpu.roll(x, (8 - k) % 8, 0) if k % 8 else x

    def picked(out, c, sets, width):
        block = out[8 * c : 8 * c + 8]
        if len(sets) == 1:
            return block
        value = block[:, :width]
        for q in sets[1:]:
            value = jnp.where(
                lax.broadcasted_iota(jnp.int32, (8, width), 0) == q,
                block[:, q * width : (q + 1) * width],
                value,
            )
        return value

    def between(rot, sets, shift):
        cols = pl.ds(sets[0] * ep, len(sets) * ep)
        parts = [
            jnp.concatenate([up(x, s + shift) for x in rot], axis=0) for s in range(3)
        ]
        near = exact_dot(jnp.concatenate(parts, axis=1), near_tab[:, cols], ((1,), (0,)))
        mine = exact_dot(parts[1], own_tab[:, cols], ((1,), (0,)))
        return mat_tmul(
            [picked(mine, c, sets, ep) for c in range(9)],
            [picked(near, c, sets, ep) for c in range(9)],
        )

    def step(rot, link, relative, live, sets):
        cols = pl.ds(sets[0] * ep, len(sets) * ep)
        tangent = log_rotation(mat_mul(link, relative))
        length = jnp.sqrt(tangent[0] * tangent[0] + tangent[1] * tangent[1] + tangent[2] * tangent[2])
        weight = live / jnp.maximum(length, min_length)
        weighed = jnp.concatenate([weight * x for x in tangent] + [weight], axis=0)
        parts = [
            exact_dot(weighed, own_tab[:, pl.ds(q * ep, ep)], ((1,), (1,))) for q in sets
        ]
        total = jnp.concatenate(parts, axis=1)
        numer = [picked(total, c, sets, scans) for c in range(3)]
        scale = 1.0 / (picked(total, 3, sets, scans) + 1.0)
        return mat_mul(rot, exp_rotation([x * scale for x in numer]))

    def padded(row):
        if ep > edges:
            row = jnp.concatenate([row, jnp.zeros((1, ep - edges), jnp.int32)], axis=1)
        return jnp.broadcast_to(row, (8, ep))

    own_lane, near_lane = padded(sch[1]), padded(nbh[1])
    side = jnp.where(near_lane >= scans, 1, 0) + jnp.where(near_lane >= 2 * scans, 1, 0)
    near_lane = near_lane - side * scans

    def taken(x, index):
        parts = [
            jnp.take_along_axis(x, index[:, 128 * i : 128 * (i + 1)], axis=1, mode="promise_in_bounds")
            for i in range(ep // 128)
        ]
        return jnp.concatenate(parts, axis=1) if len(parts) > 1 else parts[0]

    def joined(rot):
        near = []
        for x in rot:
            x = taken(x, near_lane)
            near.append(jnp.where(side == 0, pltpu.roll(x, 1, 0), jnp.where(side == 1, x, pltpu.roll(x, 7, 0))))
        return mat_tmul([taken(x, own_lane) for x in rot], near)

    first = exp_rotation([rvh[:, c, :] for c in range(3)])
    everyone = (0, 1, 2)
    link = between(first, everyone, 0)
    base = [up(x, 1) for x in first]

    @pl.when(is_mid)
    def _():
        pltpu.make_async_copy(recv1, recv1, r1).wait()
        wide = max(edges, 128)
        span = wide // edges
        lanes = m1 * n
        for q in range(KEPT // span):
            got = [recv1[pl.ds((q * span + h) * m1 + j, n, stride=block), :] for h in range(span) for j in range(m1)]
            got = jnp.concatenate(got, axis=0)
            turned_rows = [got[128 * i : 128 * (i + 1)].T for i in range(span * lanes // 128)]
            turned_rows = jnp.concatenate(turned_rows, axis=1) if len(turned_rows) > 1 else turned_rows[0]
            mine = [turned_rows[ROWS * k : ROWS * (k + 1)] for k in range(per_row)]
            owner = lax.broadcasted_iota(jnp.int32, (1, span * lanes), 1) // lanes * edges
            offset = owner.astype(F32)
            slots = lax.broadcasted_iota(jnp.int32, (wide, span * lanes), 0).astype(F32)
            table = [jnp.where(slots == x[28:29] + offset, 1.0, 0.0).astype(BF16) for x in mine]
            total = exact_dot(
                jnp.concatenate(mine, axis=1), jnp.concatenate(table, axis=1), ((1,), (1,))
            )
            for i in range(wide // 128):
                sums_ref[pl.ds(q * (wide // 128) + i, ROWS, stride=8), :] = total[:, 128 * i : 128 * (i + 1)]
        sets = KEPT * edges // 128
        h, at_t = [[None] * 6 for _ in range(6)], 0
        for x in range(6):
            for y in range(x + 1):
                h[x][y] = sums_ref[8 * at_t : 8 * at_t + 8, :] + (damping if x == y else 0.0)
                at_t += 1
        pose = [-x for x in solve(h, [sums_ref[8 * (21 + x) : 8 * (22 + x), :] for x in range(6)])]
        payload = pose + [jnp.where(sums_ref[8 * 27 : 8 * 28, :] > 0.5, 1.0, 0.0)]
        for t in range(7):
            poses[1, sets * t : sets * (t + 1), :] = payload[t][:sets]
        stacked = poses[1]

        def turned(x, by):
            if edges <= 128:
                lane = lax.rem(lax.broadcasted_iota(jnp.int32, x.shape, 1), edges)
                one = pltpu.roll(x, by, 1)
                two = pltpu.roll(x, (by - edges) % 128, 1)
                return jnp.where(lane < by, two, one)
            part = edges // 128
            row = lax.rem(lax.broadcasted_iota(jnp.int32, x.shape, 0), part)
            tall = x.shape[0]

            def moved(k):
                back = k % part
                if back == 0:
                    return x
                return jnp.where(
                    row >= back, pltpu.roll(x, back, 0), pltpu.roll(x, (back - part) % tall, 0)
                )

            lane = lax.broadcasted_iota(jnp.int32, x.shape, 1)
            whole, rest = by // 128, by % 128
            if rest == 0:
                return moved(whole)
            return jnp.where(
                lane < rest, pltpu.roll(moved(whole + 1), rest, 1), pltpu.roll(moved(whole), rest, 1)
            )

        poses[0] = turned(stacked, per * pairs)
        poses[2] = turned(stacked, edges - per * pairs)
        for q in range(sets):
            for g in range(3):
                groups[q, pl.ds(g, 8, stride=4), :] = poses[g, pl.ds(q, 8, stride=sets), :]
        held = 128 // ROWS
        for q in range(0, sets, held):
            some = range(q, min(q + held, sets))
            flat = jnp.concatenate([groups[i] for i in some], axis=0)
            if len(some) < held:
                flat = jnp.concatenate([flat, jnp.zeros((128 - ROWS * len(some), 128), F32)], axis=0)
            tab[pl.ds(128 * (q // held), 128), :] = flat.T
        for j in range(per):
            if edges <= 128:
                row = tab[pl.ds(j, n, stride=per), :]
                for h2 in range(1, span):
                    row = row + pltpu.roll(tab[pl.ds(h2 * edges + j, n, stride=per), :], ROWS * sets * h2, 1)
                send2[:, j, 0, :] = row
            else:
                part = edges // 128
                count = 128 // per
                for i in range(sets // held):
                    strip = tab[pl.ds(128 * i + j, count, stride=per), :]
                    for b in range(part):
                        send2[pl.ds(b * count, count), j, i, :] = pltpu.roll(strip, (128 - ROWS * b) % 128, 1)
        each_other(
            lambda to, where: pltpu.make_async_remote_copy(
                send2.at[to], recv2.at[rank], s2, r2, device_id=where, device_id_type=MESH
            ).start()
        )
        pltpu.make_async_copy(send2.at[me], recv2.at[rank], r2).start()

    pltpu.make_async_copy(recv2, recv2, r2).wait()
    part = max(edges // 128, 1)
    span = max(128 // edges, 1)
    sets = KEPT * edges // 128
    for o in range(KEPT):
        lane, row = (ROWS * (o % span * sets + o // span), 0) if edges <= 128 else (ROWS * part * o, 0)
        row, lane = lane // 128, lane % 128
        for j in range(per):
            rows2[pl.ds(per * o + j, len(mids), stride=per * KEPT), :] = pltpu.roll(
                recv2[:, j, row, :], (128 - lane) % 128, 1
            ) if lane else recv2[:, j, row, :]
    back = [rows2[pl.ds(128 * i, 128), :].T for i in range(ep // 128)]
    back = jnp.concatenate(back, axis=1) if len(back) > 1 else back[0]
    comp = []
    for t in range(7):
        tile = back[8 * (t // 2) : 8 * (t // 2) + 8]
        comp.append(pltpu.roll(tile, 4, 0) if t % 2 else tile)
    for t in range(6):
        pose_ref[t : t + 1, :] = comp[t][1:2, :edges]
    relative = exp_rotation(comp[:3])
    second = step(base, link, relative, comp[6], everyone)
    link = joined(second) if scans == 128 else between(second, (1,), -1)
    final = step(second, link, relative, comp[6], (1,))
    for c in range(9):
        rot_ref[c : c + 1, :] = final[c][1:2]

    @pl.when(is_mid)
    def _():
        sent = send1.at[pl.ds(0, n * m1 - block)]
        pltpu.make_async_copy(sent, sent, s1).wait()
        sent = send2.at[pl.ds(0, n - 1)]
        pltpu.make_async_copy(sent, sent, s2).wait()

    @pl.when(jnp.logical_not(is_mid))
    def _():
        pltpu.make_async_copy(send1, send1, s1).wait()

    pltpu.make_async_copy(rvh.at[pl.ds(0, 4)], rvh.at[pl.ds(0, 4)], hs).wait()
    pltpu.make_async_copy(sch.at[pl.ds(0, 2)], sch.at[pl.ds(0, 2)], es).wait()
    pltpu.make_async_copy(nbh.at[pl.ds(0, 2)], nbh.at[pl.ds(0, 2)], ns).wait()


def finish(pose_ref, rot_ref, pose_out, rot_out, sems):
    copies = [
        pltpu.make_async_copy(pose_ref, pose_out, sems.at[0]),
        pltpu.make_async_copy(rot_ref, rot_out, sems.at[1]),
    ]
    for copy in copies:
        copy.start()
    for copy in copies:
        copy.wait()


def solution(mesh):
    regions, pairs = mesh.shape["region"], mesh.shape["pair"]
    n = regions * pairs

    def on_device(points, offsets, normals, block_count, block_edge, edge_scan, edge_nbr, rotvec):
        blocks, edges, scans = points.shape[1], edge_scan.shape[0], rotvec.shape[1]
        slot, per = blocks // n, edges // n
        m1 = slot * ROWS // 128
        ep = max(edges, 128)
        sets = KEPT * edges // 128
        lines = max(edges // 128, 1)
        dma = pltpu.SemaphoreType.DMA
        vm = pl.BlockSpec(memory_space=pltpu.VMEM)
        hbm = pl.BlockSpec(memory_space=pl.ANY)
        pose, rot = pl.pallas_call(
            functools.partial(kernel, (regions, pairs, blocks, edges, scans)),
            out_shape=(pltpu.VMEM((6, edges), F32), pltpu.VMEM((9, scans), F32)),
            in_specs=[hbm] * 8,
            out_specs=(vm, vm),
            scratch_shapes=[
                pltpu.VMEM((blocks // 128, 3, 3, 128, 128), F32),
                pltpu.VMEM((2, 9, 128, 128), F32),
                pltpu.VMEM((8 * ROWS, 128), F32),
                pltpu.VMEM((max(blocks, KEPT * edges), 128), F32),
                pltpu.VMEM((n * m1, 128), F32),
                pltpu.VMEM((n * KEPT * m1, 128), F32),
                pltpu.VMEM((8 * ROWS, 128), F32),
                pltpu.VMEM((3, 8 * sets, 128), F32),
                pltpu.VMEM((sets, ROWS, 128), F32),
                pltpu.VMEM((n, per, lines, 128), F32),
                pltpu.VMEM((n // KEPT, per, lines, 128), F32),
                pltpu.VMEM((ep, 128), F32),
                pltpu.VMEM((8, 3, scans), F32),
                pltpu.VMEM((3, 1, edges), jnp.int32),
                pltpu.VMEM((3, 1, edges), jnp.int32),
                pltpu.VMEM((3 * scans, 3 * ep), BF16),
                pltpu.VMEM((scans, 3 * ep), BF16),
                pltpu.VMEM((1, blocks), jnp.int32),
                pltpu.VMEM((1, blocks), jnp.int32),
                dma((blocks // 128, 3)),
                dma((2,)),
                dma, dma, dma, dma, dma, dma, dma, dma, dma, dma,
            ],
            compiler_params=pltpu.CompilerParams(collective_id=0, has_side_effects=True),
        )(
            points, offsets, normals, block_count[None], block_edge[None],
            edge_scan[None], edge_nbr[None], rotvec,
        )
        return pl.pallas_call(
            finish,
            out_shape=(
                jax.ShapeDtypeStruct((6, edges), F32),
                jax.ShapeDtypeStruct((9, scans), F32),
            ),
            in_specs=[vm] * 2,
            out_specs=(hbm, hbm),
            scratch_shapes=[dma((2,))],
        )(*(pltpu.with_memory_space_constraint(x, pltpu.VMEM) for x in (pose, rot)))

    flat = P(("region", "pair"))
    cut = P(None, ("region", "pair"))
    return jax.shard_map(
        on_device,
        mesh=mesh,
        in_specs=(P(None, ("region", "pair"), None),) * 3 + (flat,) * 4 + (cut,),
        out_specs=(cut, cut),
        check_vma=False,
    )
```
